32 devices in a mesh: groups: 2 (over y), dom: 4 (over x, core), subj: 4 (over z).
Axes of the slice: x: 2, y: 2, z: 4, core: 2. Of those that a mesh axis runs over, the one named last changes fastest.
Arguments:
- image: float32 [8, 32, 64, 256], P(('groups', 'subj'), 'dom'), parts along dimension 0, may hold values from -6 to 6
- velocity: float32 [8, 3, 32, 64, 256], P(('groups', 'subj'), None, 'dom'), parts along dimension 0, may hold values from -4 to 4
- template: float32 [64, 64, 256], P(('groups', 'dom'), 'subj'), parts along dimension 0, may hold values from -6 to 6
- foreground: int32 [8, 32, 8, 16], P(('groups', 'subj'), 'dom'), parts along dimension 0, may hold values 0 or 1
- assignment: int32 [8], P('groups'), parts along dimension 0, may hold values from 0 to 3, each once
- subj_weight: float32 [8], P('groups'), parts along dimension 0, may hold values from 0.25 to 4
Outputs:
- new_template: float32 [64, 64, 256], P(('groups', 'dom'), 'subj'), parts along dimension 0
- residual: float32 [8, 32, 64, 256], P(('groups', 'subj'), 'dom'), parts along dimension 0
The draws below stay inside these ranges and needn't reach their ends.
There are 2 independent parts, one for each index of `groups`. The reference program is written for one: setup_inputs(seed, part) draws one part's arguments, and reference() takes and returns one part's arrays. A program takes and returns all parts, laid end to end along the dimension named above; each array names one. Nothing has to cross between parts.
All inputs are finite; a program needn't handle non-finite values. No bound on the sum of `foreground` on one device may be relied on, other than what follows from the above.
Results may differ from the reference program's by a relative error of at most 0.00002.
Values sent between devices are 32-bit elements; how exact they have to be, the bound alone decides.
A program may use at most 64 MiB of HBM per device.

```python
import math
import jax
import jax.numpy as jnp
from jax import lax

CY = 64
CX = 256
NSTEP = 4
BLOCK_Y = 8
BLOCK_X = 16
NZ = 32
SUBJECTS = 4


def touch_ends(values, key, low, top_value):
    index_at = [jax.random.randint(jax.random.fold_in(key, axis), (), 0, length) for axis, length in enumerate(values.shape)]
    widest = values.shape.index(max(values.shape))
    next_to = index_at[:widest] + [(index_at[widest] + 1) % values.shape[widest]] + index_at[widest + 1:]
    return values.at[tuple(index_at)].set(low).at[tuple(next_to)].set(top_value)


def level_of(own_key, shape, cuts, low, largest):
    factor_of = 1.0
    for axis_at, shards_of in cuts:
        heights = jax.random.uniform(jax.random.fold_in(jax.random.fold_in(own_key, 6), axis_at), (shards_of,), jnp.float32, low / len(cuts), largest / len(cuts))
        factor_of = factor_of * jnp.repeat(jnp.exp(heights), shape[axis_at] // shards_of).reshape((-1,) + (1,) * (len(shape) - 1 - axis_at))
    return factor_of


def noise(rng, shape, deviation, reach, shards=(), kind=jnp.bfloat16):
    loudness = level_of(rng, shape, shards, -0.22, 0.18) if shards else 1.0
    drawn = jax.random.normal(rng, shape, jnp.float32) * deviation * loudness
    return jnp.minimum(jnp.maximum(drawn, -reach), reach).astype(kind)


def setup_inputs(seed: int = 0, part: int = 0) -> dict:
    streams_of = jax.random.split(jax.random.key(seed), 7)
    part_splits = jax.random.split(jax.random.fold_in(streams_of[6], part), 7)
    return {
        "image": noise(part_splits[0], (SUBJECTS, NZ, CY, CX), 1.0, 6.0, ((0, 4), (1, 4)), jnp.float32),
        "velocity": noise(part_splits[1], (SUBJECTS, 3, NZ, CY, CX), 1.0, 4.0, ((0, 4), (2, 4)), jnp.float32),
        "template": noise(part_splits[2], (NZ, CY, CX), 1.0, 6.0, ((0, 4), (1, 4)), jnp.float32),
        "foreground": touch_ends((jax.random.randint(part_splits[3], (SUBJECTS, NZ, CY // BLOCK_Y, CX // BLOCK_X), 0, 4) < 3).astype(jnp.int32), jax.random.fold_in(part_splits[3], 1), 0, 1),
        "assignment": jax.random.permutation(part_splits[4], SUBJECTS).astype(jnp.int32),
        "subj_weight": jnp.clip(jnp.exp(jax.random.uniform(part_splits[5], (SUBJECTS,), jnp.float32, math.log(0.25), math.log(4.0))), 0.25, 4.0),
    }


STEP_DT = 0.25


def central(field, axis):
    pads = [(0, 0)] * field.ndim
    pads[axis] = (1, 1)
    padded = jnp.pad(field, pads)
    length = padded.shape[axis]
    upper = lax.slice_in_dim(padded, 2, length, axis=axis)
    lower = lax.slice_in_dim(padded, 0, length - 2, axis=axis)
    return 0.5 * (upper - lower)


def expand(flags):
    depth, rows, cols = flags.shape
    grown = jnp.broadcast_to(flags[:, :, None, :, None], (depth, rows, BLOCK_Y, cols, BLOCK_X))
    return grown.reshape(depth, rows * BLOCK_Y, cols * BLOCK_X).astype(jnp.float32)


def forward_step(field, flow):
    return field - STEP_DT * (flow[0] * central(field, 0) + flow[1] * central(field, 1) + flow[2] * central(field, 2))


def adjoint_step(field, flow):
    return field + STEP_DT * (central(flow[0] * field, 0) + central(flow[1] * field, 1) + central(flow[2] * field, 2))


def reference(image, velocity, template, foreground, assignment, subj_weight):
    total = jnp.sum(subj_weight)
    gradient = jnp.zeros_like(template)
    outputs = []
    for slot in range(SUBJECTS):
        flow = velocity[slot]
        warped = template
        for step in range(NSTEP):
            warped = forward_step(warped, flow)
        weight = subj_weight[assignment[slot]]
        resid = weight * expand(foreground[slot]) * (warped - image[slot])
        outputs.append(resid)
        costate = resid
        for step in range(NSTEP):
            costate = adjoint_step(costate, flow)
        gradient = gradient + costate
    new_template = template - gradient / total
    return new_template, jnp.stack(outputs)
```

```python
import functools

import jax
import jax.numpy as jnp
from jax import lax
from jax.experimental import pallas as pl
from jax.experimental.pallas import tpu as pltpu
from jax.sharding import PartitionSpec as P

BLOCK_Y = 8
BLOCK_X = 16
MESH = pl.DeviceIdType.MESH
F32 = jnp.float32
SCALE = 0.125


def kernel(
    nd, ns,
    asg, sw, fg, img_h, vel_h, tmp_h,
    new_h, res_h,
    gbuf, hbuf, vel, img, mask, fld, cst, flx, tiles, rbl, rbr, sbl, sbr, newv,
    lsem, gss, gsr, hss, hsr, vss, vsr, ess, esr, rss, rsr,
):
    d = lax.axis_index("dom")
    s = lax.axis_index("subj")
    nz, rows_t, cx = tmp_h.shape
    cy = img_h.shape[2]
    e = nz + 2

    has = {
        ("dom", -1): d > 0,
        ("dom", 1): d < nd - 1,
        ("subj", -1): s > 0,
        ("subj", 1): s < ns - 1,
    }

    def remote(src, dst, ssem, rsem, axis, step):
        here = d if axis == "dom" else s
        return pltpu.make_async_remote_copy(
            src_ref=src, dst_ref=dst, send_sem=ssem, recv_sem=rsem,
            device_id={axis: here + step}, device_id_type=MESH,
        )

    c_tmp = pltpu.make_async_copy(tmp_h, gbuf.at[s], lsem.at[0])
    c_vel = pltpu.make_async_copy(vel_h.at[0], vel.at[:, pl.ds(1, nz)], lsem.at[1])
    c_img = pltpu.make_async_copy(img_h.at[0], img, lsem.at[2])
    c_tmp.start()
    c_vel.start()
    c_img.start()

    barrier = pltpu.get_barrier_semaphore()
    for (axis, step), there in has.items():
        @pl.when(there)
        def _(axis=axis, step=step):
            here = d if axis == "dom" else s
            pl.semaphore_signal(barrier, inc=1, device_id={axis: here + step}, device_id_type=MESH)
    count = sum(jnp.where(there, 1, 0) for there in has.values())
    pl.semaphore_wait(barrier, count)

    def halo_copy(t, step):
        side = 1 if step < 0 else 0
        src = gbuf.at[t, pl.ds(0, 2)] if step < 0 else gbuf.at[t, pl.ds(nz - 2, 2)]
        return remote(src, hbuf.at[side, t], hss.at[side, t], hsr.at[side, t], "dom", step)

    def halo_send(t):
        for step in (-1, 1):
            @pl.when(has["dom", step])
            def _(step=step):
                halo_copy(t, step).start()

    def tile_copy(h, step):
        t = s - h if step > 0 else s + h
        k = 0 if step > 0 else 1
        return remote(gbuf.at[t], gbuf.at[t], gss.at[k, h], gsr.at[k, h], "subj", step)

    def vel_copy(step):
        side = 1 if step < 0 else 0
        src = vel.at[:, pl.ds(1, 1)] if step < 0 else vel.at[:, pl.ds(nz, 1)]
        dst = vel.at[:, pl.ds(nz + 1, 1)] if step < 0 else vel.at[:, pl.ds(0, 1)]
        return remote(src, dst, vss.at[side], vsr.at[side], "dom", step)

    c_tmp.wait()
    for step in (1, -1):
        @pl.when(has["subj", step])
        def _(step=step):
            tile_copy(0, step).start()
    halo_send(s)

    c_vel.wait()
    for step in (-1, 1):
        @pl.when(has["dom", step])
        def _(step=step):
            vel_copy(step).start()

    @pl.when(d == 0)
    def _():
        hbuf[0] = jnp.zeros(hbuf.shape[1:], F32)
        vel[:, 0] = jnp.zeros((3, cy, cx), F32)
        fld[2, 0:2] = jnp.zeros((2, cy, cx), F32)
        for k in (0, 2):
            cst[k, 1] = jnp.zeros((cy, cx), F32)
            flx[k, 0] = jnp.zeros((cy, cx), F32)

    @pl.when(d == nd - 1)
    def _():
        hbuf[1] = jnp.zeros(hbuf.shape[1:], F32)
        vel[:, nz + 1] = jnp.zeros((3, cy, cx), F32)
        fld[2, e:e + 2] = jnp.zeros((2, cy, cx), F32)
        for k in (0, 2):
            cst[k, e] = jnp.zeros((cy, cx), F32)
            flx[k, e + 1] = jnp.zeros((cy, cx), F32)

    weight = sw[asg[s]]
    total = sw[0]
    for i in range(1, ns):
        total = total + sw[i]
    by = cy // BLOCK_Y
    bx = cx // BLOCK_X
    spread_x = (
        lax.broadcasted_iota(jnp.int32, (bx, cx), 1) // BLOCK_X
        == lax.broadcasted_iota(jnp.int32, (bx, cx), 0)
    ).astype(F32)
    spread_y = (
        lax.broadcasted_iota(jnp.int32, (cy, by), 0) // BLOCK_Y
        == lax.broadcasted_iota(jnp.int32, (cy, by), 1)
    ).astype(F32)

    def mask_plane(z, _):
        flags = fg[0, z].astype(F32)
        wide = jnp.dot(flags, spread_x, preferred_element_type=F32)
        mask[z] = weight * jnp.dot(spread_y, wide, preferred_element_type=F32)
        return 0

    lax.fori_loop(0, nz, mask_plane, 0)

    for h in range(1, ns):
        for step in (1, -1):
            t = s - h if step > 0 else s + h
            inside = (s >= h) if step > 0 else (s + h <= ns - 1)

            @pl.when(inside)
            def _(h=h, step=step, t=t):
                k = 0 if step > 0 else 1
                remote(gbuf.at[t], gbuf.at[t], gss.at[k, h - 1], gsr.at[k, h - 1], "subj", step).wait_recv()
                if h < ns - 1:
                    @pl.when(has["subj", step])
                    def _():
                        tile_copy(h, step).start()
                halo_send(t)

    for t in range(ns):
        fld[0, 2:e, t * rows_t:(t + 1) * rows_t, :] = gbuf[t]
    for step in (-1, 1):
        @pl.when(has["dom", -step])
        def _(step=step):
            for t in range(ns):
                halo_copy(t, step).wait_recv()
            vel_copy(step).wait_recv()
    for t in range(ns):
        fld[0, 0:2, t * rows_t:(t + 1) * rows_t, :] = hbuf[0, t]
        fld[0, e:e + 2, t * rows_t:(t + 1) * rows_t, :] = hbuf[1, t]

    row = lax.broadcasted_iota(jnp.int32, (cy, cx), 0)
    col = lax.broadcasted_iota(jnp.int32, (cy, cx), 1)

    def diff(f, axis):
        at, length = (row, cy) if axis == 0 else (col, cx)
        upper = jnp.where(at == length - 1, 0.0, pltpu.roll(f, length - 1, axis))
        lower = jnp.where(at == 0, 0.0, pltpu.roll(f, 1, axis))
        return upper - lower

    def planes(lo, hi, body):
        def step(z, _):
            body(z)
            return 0
        lax.fori_loop(lo, hi, step, 0)

    def forward(k, z):
        f = fld[k, z]
        return f - SCALE * (
            vel[0, z - 1] * (fld[k, z + 1] - fld[k, z - 1])
            + vel[1, z - 1] * diff(f, 0)
            + vel[2, z - 1] * diff(f, 1)
        )

    def forward_to(k):
        def body(z):
            fld[k + 1, z] = forward(k, z)
        return body

    def residual(z):
        r = mask[z - 2] * (forward(3, z) - img[z - 2])
        cst[0, z] = r
        flx[0, z] = vel[0, z - 1] * r

    def adjoint(k, z):
        g = cst[k, z]
        return g + SCALE * (
            flx[k, z + 1] - flx[k, z - 1]
            + diff(vel[1, z - 1] * g, 0)
            + diff(vel[2, z - 1] * g, 1)
        )

    def adjoint_to(k):
        def body(z):
            g = adjoint(k, z)
            cst[k + 1, z] = g
            flx[k + 1, z] = vel[0, z - 1] * g
        return body

    def last(z):
        g = adjoint(3, z)
        for t in range(ns):
            tiles[t, z - 2] = g[t * rows_t:(t + 1) * rows_t, :]

    def edge_copies(k, step):
        side = 1 if step < 0 else 0
        if k == 0:
            src = fld.at[2, pl.ds(2, 2)] if step < 0 else fld.at[2, pl.ds(e - 2, 2)]
            dst = fld.at[2, pl.ds(e, 2)] if step < 0 else fld.at[2, pl.ds(0, 2)]
            pairs = [(src, dst)]
        else:
            j = 2 * (k - 1)
            if step < 0:
                pairs = [(cst.at[j, 2], cst.at[j, e]), (flx.at[j, 3], flx.at[j, e + 1])]
            else:
                pairs = [(cst.at[j, e - 1], cst.at[j, 1]), (flx.at[j, e - 2], flx.at[j, 0])]
        return [
            remote(src, dst, ess.at[k, side, i], esr.at[k, side, i], "dom", step)
            for i, (src, dst) in enumerate(pairs)
        ]

    def edge_send(k):
        for step in (-1, 1):
            @pl.when(has["dom", step])
            def _(step=step):
                for c in edge_copies(k, step):
                    c.start()

    def edge_wait(k):
        for step in (-1, 1):
            @pl.when(has["dom", -step])
            def _(step=step):
                for c in edge_copies(k, step):
                    c.wait_recv()

    def second(k, body):
        planes(2, 4, body)
        planes(e - 2, e, body)
        edge_send(k)
        planes(4, e - 2, body)

    def first(k, body, pre=None):
        planes(3, e - 1, body)
        edge_wait(k)
        if pre is not None:
            pre()
        planes(1, 3, body)
        planes(e - 1, e + 1, body)

    def outer_flux(k):
        def go():
            flx[k, 1] = vel[0, 0] * cst[k, 1]
            flx[k, e] = vel[0, nz + 1] * cst[k, e]
        return go

    planes(1, e + 1, forward_to(0))
    second(0, forward_to(1))
    first(0, forward_to(2))
    c_img.wait()
    second(1, residual)
    c_res = pltpu.make_async_copy(cst.at[0, pl.ds(2, nz)], res_h.at[0], lsem.at[3])
    c_res.start()
    first(1, adjoint_to(0), outer_flux(0))
    second(2, adjoint_to(1))
    first(2, adjoint_to(2), outer_flux(2))
    planes(2, e, last)

    def sum_copy(t, step):
        k = 0 if step > 0 else 1
        sb, rb = (sbr, rbr) if step > 0 else (sbl, rbl)
        return remote(sb.at[t], rb.at[t], rss.at[k, t], rsr.at[k, t], "subj", step)

    def sum_step(t, step):
        sb, rb = (sbr, rbr) if step > 0 else (sbl, rbl)
        first_one = (s == 0) if step > 0 else (s == ns - 1)
        before = (s < t) if step > 0 else (s > t)
        within = (s <= t) if step > 0 else (s >= t)

        @pl.when(within & jnp.logical_not(first_one))
        def _():
            sum_copy(t, step).wait_recv()

        @pl.when(before & first_one)
        def _():
            sb[t] = tiles[t]
            sum_copy(t, step).start()

        @pl.when(before & jnp.logical_not(first_one))
        def _():
            sb[t] = tiles[t] + rb[t]
            sum_copy(t, step).start()

    @pl.when(s < ns // 2)
    def _():
        for t in range(ns):
            sum_step(ns - 1 - t, 1)
            sum_step(t, -1)

    @pl.when(s >= ns // 2)
    def _():
        for t in range(ns):
            sum_step(t, -1)
            sum_step(ns - 1 - t, 1)

    newv[...] = tiles[s]

    @pl.when(s > 0)
    def _():
        newv[...] += rbr[s]

    @pl.when(s < ns - 1)
    def _():
        newv[...] += rbl[s]

    newv[...] = gbuf[s] - newv[...] / jnp.full((nz, rows_t, cx), total, F32)
    c_new = pltpu.make_async_copy(newv, new_h, lsem.at[4])
    c_new.start()

    for step in (-1, 1):
        @pl.when(has["dom", step])
        def _(step=step):
            for t in range(ns):
                halo_copy(t, step).wait_send()
            vel_copy(step).wait_send()
            for k in range(3):
                for c in edge_copies(k, step):
                    c.wait_send()

        @pl.when(has["subj", step])
        def _(step=step):
            for h in range(ns - 1):
                @pl.when((s >= h) if step > 0 else (s + h <= ns - 1))
                def _(h=h):
                    tile_copy(h, step).wait_send()
            for t in range(ns):
                @pl.when((s < t) if step > 0 else (s > t))
                def _(t=t):
                    sum_copy(t, step).wait_send()
    c_res.wait()
    c_new.wait()


def local(nd, ns, image, velocity, template, foreground, assignment, subj_weight):
    nz, rows_t, cx = template.shape
    cy = image.shape[2]
    vmem = lambda *shape: pltpu.VMEM(shape, F32)
    dma = lambda *shape: pltpu.SemaphoreType.DMA(shape)
    any_spec = pl.BlockSpec(memory_space=pl.ANY)
    smem_spec = pl.BlockSpec(memory_space=pltpu.SMEM)
    return pl.pallas_call(
        functools.partial(kernel, nd, ns),
        out_shape=(
            jax.ShapeDtypeStruct(template.shape, F32),
            jax.ShapeDtypeStruct(image.shape, F32),
        ),
        in_specs=[smem_spec, smem_spec, pl.BlockSpec(memory_space=pltpu.VMEM), any_spec, any_spec, any_spec],
        out_specs=(any_spec, any_spec),
        scratch_shapes=[
            vmem(ns, nz, rows_t, cx),
            vmem(2, ns, 2, rows_t, cx),
            vmem(3, nz + 2, cy, cx),
            vmem(nz, cy, cx),
            vmem(nz, cy, cx),
            vmem(4, nz + 4, cy, cx),
            vmem(4, nz + 4, cy, cx),
            vmem(4, nz + 4, cy, cx),
            vmem(ns, nz, rows_t, cx),
            vmem(ns, nz, rows_t, cx),
            vmem(ns, nz, rows_t, cx),
            vmem(ns, nz, rows_t, cx),
            vmem(ns, nz, rows_t, cx),
            vmem(nz, rows_t, cx),
            dma(5),
            dma(2, ns), dma(2, ns),
            dma(2, ns), dma(2, ns),
            dma(2), dma(2),
            dma(3, 2, 2), dma(3, 2, 2),
            dma(2, ns), dma(2, ns),
        ],
        compiler_params=pltpu.CompilerParams(
            collective_id=0, has_side_effects=True, vmem_limit_bytes=32 * 1024 * 1024
        ),
    )(assignment, subj_weight, foreground, image, velocity, template)


def solution(mesh):
    in_specs = (
        P(("groups", "subj"), "dom", None, None),
        P(("groups", "subj"), None, "dom", None, None),
        P(("groups", "dom"), "subj", None),
        P(("groups", "subj"), "dom", None, None),
        P("groups"),
        P("groups"),
    )
    out_specs = (P(("groups", "dom"), "subj", None), P(("groups", "subj"), "dom", None, None))
    body = functools.partial(local, mesh.shape["dom"], mesh.shape["subj"])
    return jax.shard_map(body, mesh=mesh, in_specs=in_specs, out_specs=out_specs, check_vma=False)
```
